256 devices in a mesh: chan: 16 (over z, y_lo), tm: 16 (over x, y_hi, core).
Axes of the slice: x: 4, y: 4 (y_hi: 2, y_lo: 2; y = y_hi * 2 + y_lo), z: 8, core: 2. Of those that a mesh axis runs over, the one named last changes fastest.
Arguments:
- raw: float32 [2, 512, 4096], P(None, 'chan', 'tm'), may hold values from -40 to 40
- alive: int32 [512], P(('chan', 'tm')), may hold values 0 or 1
- seg_start: int32 [2], replicated, may hold values from 0 to 256, as said below
- norm_half: int32 [512], P(('chan', 'tm')), may hold values from 32 to 64, as said below
Outputs:
- corr: bfloat16 [512, 129, 512], P(('chan', 'tm'))
The draws below stay inside these ranges and needn't reach their ends.
Inputs may be any that keep to these rules, and one draw needn't show every extreme that they name: `seg_start`: some segment starts exactly 256 samples into its window. `norm_half`: some channel has half-length 32 and some 64.
All inputs are finite; a program needn't handle non-finite values. No bound on the sum of `alive` on one device may be relied on, other than what follows from the above.
Results may differ from the reference program's by a relative error of at most 0.02.
Values may be sent and summed in bfloat16 or wider, within the bound.
No kernel may reach another device: no remote copies, remote signals or barrier semaphores. Data moves between devices by JAX's collectives and lax.ppermute only.
A program may use at most 64 MiB of HBM per device.

```python
import math
import jax
import jax.numpy as jnp
from jax import lax

CH_DEV = 32
T_DEV = 256
SEGS = 2
LAG = 64
C = 512
NT = 4096
BAND_LO = 16
BAND_HI = 1638


def draw_raw(key, part):
    key_noise, key_level = jax.random.split(jax.random.fold_in(key, 11), 2)
    block_count = NT // 64
    noise = jnp.clip(jax.random.normal(key_noise, (SEGS, C, NT), jnp.float32), -4.0, 4.0)
    level = jax.random.uniform(key_level, (SEGS, C, block_count), jnp.float32, -2.3, 2.3)
    envelope = jnp.repeat(jnp.exp(level), 64, axis=2)
    return noise * envelope


def draw_seg_start(key, part):
    key_pick, key_value = jax.random.split(jax.random.fold_in(key, 23))
    values = jax.random.randint(key_value, (SEGS,), 0, T_DEV + 1)
    chosen = jax.random.randint(key_pick, (), 0, SEGS)
    return jnp.where(jnp.arange(SEGS) == chosen, T_DEV, values).astype(jnp.int32)


def draw_norm_half(key, part):
    key_value, key_first, key_second = jax.random.split(jax.random.fold_in(key, 37), 3)
    values = jax.random.randint(key_value, (C,), 32, 65)
    top_slot = jax.random.randint(key_first, (), 0, C)
    low_slot = (top_slot + 1 + jax.random.randint(key_second, (), 0, C - 1)) % C
    positions = jnp.arange(C)
    values = jnp.where(positions == top_slot, 64, values)
    values = jnp.where(positions == low_slot, 32, values)
    return values.astype(jnp.int32)


def plant(array, own_key, smallest, largest):
    place = [jax.random.randint(jax.random.fold_in(own_key, axis), (), 0, length) for axis, length in enumerate(array.shape)]
    main_axis = array.shape.index(max(array.shape))
    next_to = place[:main_axis] + [(place[main_axis] + 1) % array.shape[main_axis]] + place[main_axis + 1:]
    return array.at[tuple(place)].set(smallest).at[tuple(next_to)].set(largest)


def setup_inputs(seed: int = 0) -> dict:
    splits = jax.random.split(jax.random.key(seed), 5)
    raw = draw_raw(jax.random.fold_in(splits[4], 71), 0)
    alive = plant((jax.random.randint(splits[1], (C,), 0, 16) < 15).astype(jnp.int32), jax.random.fold_in(splits[1], 1), 0, 1)
    seg_start = draw_seg_start(jax.random.fold_in(splits[4], 71), 0)
    norm_half = draw_norm_half(jax.random.fold_in(splits[4], 71), 0)
    return {"raw": raw, "alive": alive, "seg_start": seg_start, "norm_half": norm_half}


widest = 64
smooth_half = 32
tiny = 1e-05

def window_mean(signal, half_width):
    length = signal.shape[2]
    padded = jnp.pad(jnp.abs(signal), ((0, 0), (0, 0), (widest, widest)))
    running = jnp.cumsum(padded, axis=2)
    running = jnp.concatenate([jnp.zeros(running.shape[:2] + (1,), jnp.float32), running], axis=2)
    moments = jnp.arange(length, dtype=jnp.int32)
    full_shape = signal.shape
    upper_index = jnp.broadcast_to(moments[None, None, :] + half_width[None, :, None] + 1 + widest, full_shape).astype(jnp.int32)
    lower_index = jnp.broadcast_to(moments[None, None, :] - half_width[None, :, None] + widest, full_shape).astype(jnp.int32)
    total = jnp.take_along_axis(running, upper_index, axis=2) - jnp.take_along_axis(running, lower_index, axis=2)
    return total / (2 * half_width[None, :, None] + 1).astype(jnp.float32)

def reference(raw, alive, seg_start, norm_half):
    masked = raw * alive.astype(jnp.float32)[None, :, None]
    pieces = []
    for segment in range(SEGS):
        padded = jnp.pad(masked[segment], ((0, 0), (0, NT)))
        pieces.append(lax.dynamic_slice_in_dim(padded, seg_start[segment].astype(jnp.int32), NT, axis=1))
    signal = jnp.stack(pieces, axis=0)
    level = window_mean(signal, norm_half.astype(jnp.int32))
    normed = signal / (level + tiny)
    spectrum = jnp.fft.rfft(normed, axis=2)
    magnitude = jnp.abs(spectrum)
    reflected = jnp.pad(magnitude, ((0, 0), (0, 0), (smooth_half, smooth_half)), mode='reflect')
    running = jnp.cumsum(reflected, axis=2)
    running = jnp.concatenate([jnp.zeros(running.shape[:2] + (1,), jnp.float32), running], axis=2)
    span_bins = 2 * smooth_half + 1
    smooth = (running[:, :, span_bins:] - running[:, :, :-span_bins]) / span_bins
    bins = jnp.arange(NT // 2 + 1, dtype=jnp.int32)
    band = ((bins >= BAND_LO) & (bins <= BAND_HI)).astype(jnp.float32)
    gain = band[None, None, :] / (smooth + tiny)
    white = (jnp.fft.irfft(spectrum * gain, n=NT, axis=2) * math.sqrt(NT)).astype(jnp.bfloat16)
    wide = white.astype(jnp.float32)
    padded_all = jnp.pad(wide, ((0, 0), (0, 0), (LAG, LAG)))
    block_count = C // CH_DEV
    blocked = jnp.transpose(padded_all.reshape(SEGS, block_count, CH_DEV, NT + 2 * LAG), (1, 0, 2, 3))

    def one_block(block_rows):
        toeplitz = jnp.stack([block_rows[:, :, 2 * LAG - offset:2 * LAG - offset + NT] for offset in range(2 * LAG + 1)], axis=2)
        return jnp.einsum('silu,sju->ilj', toeplitz, wide, precision=lax.Precision.HIGHEST)
    totals = lax.map(one_block, blocked).reshape(C, 2 * LAG + 1, C)
    scaled = totals * (1.0 / math.sqrt(SEGS * NT))
    channel_ids = jnp.arange(C, dtype=jnp.int32)
    keep = channel_ids[:, None, None] != channel_ids[None, None, :]
    return jnp.where(keep, scaled, 0.0).astype(jnp.bfloat16)
```

```python
import functools
import math

import jax
import jax.numpy as jnp
import ml_dtypes
import numpy as np
from jax import lax
from jax.experimental import pallas as pl
from jax.experimental.pallas import tpu as pltpu
from jax.sharding import PartitionSpec as P

LAG = 64
TINY = 1e-05
NT = 4096
Q = 32
GROUPS = 4
LINE = 2 * (NT + LAG)
STEP = 16
A_BLOCKS = 2 * LAG // STEP
CHUNK = 13 * 128
BAND_LO = 16
BAND_HI = 1638
BINS = 64

bf16 = jnp.bfloat16
f32 = jnp.float32


def split_const(table):
    high = table.astype(ml_dtypes.bfloat16)
    low = (table - high.astype(np.float64)).astype(ml_dtypes.bfloat16)
    return high, low


@functools.lru_cache(maxsize=None)
def tables():
    q = np.arange(Q)
    p = np.arange(128)
    eye = np.eye(GROUPS)
    ang_q = 2 * np.pi * np.outer(q, q) / Q
    cos_q, sin_q = np.kron(eye, np.cos(ang_q)), np.kron(eye, np.sin(ang_q))
    first = np.concatenate([cos_q, -sin_q], axis=0)
    last = np.concatenate([cos_q, -sin_q], axis=1)
    ang_t = 2 * np.pi * np.outer(q, p) / NT
    twiddle = np.concatenate([np.tile(np.cos(ang_t), (GROUPS, 1)), np.tile(np.sin(ang_t), (GROUPS, 1))], axis=0)
    ang_p = 2 * np.pi * np.outer(p, np.arange(BINS) - 1) / 128
    cos_p, sin_p = np.cos(ang_p), np.sin(ang_p)
    second = np.block([[cos_p, -sin_p], [sin_p, cos_p]])
    third = np.block([[cos_p.T, sin_p.T], [-sin_p.T, cos_p.T]])
    tri = np.concatenate([
        np.kron(eye, np.ones((Q, Q))),
        np.kron(eye, (q[None, :] >= q[:, None]).astype(float)),
        np.kron(eye, (q[None, :] <= q[:, None]).astype(float)),
    ], axis=0)
    out = []
    for table in (first, second, third, last):
        out.extend(split_const(table))
    out.append(tri.astype(ml_dtypes.bfloat16))
    out.append(twiddle.astype(np.float32))
    return out


def parts2(x):
    high = x.astype(bf16)
    return high, (x - high.astype(f32)).astype(bf16)


def parts3(x):
    high = x.astype(bf16)
    rest = x - high.astype(f32)
    mid = rest.astype(bf16)
    return high, mid, (rest - mid.astype(f32)).astype(bf16)


def dot(a, b):
    return jnp.dot(a, b, preferred_element_type=f32)


def right_product(x, high, low):
    xh, xl = parts2(x)
    return dot(xh, high) + (dot(xl, high) + dot(xh, low))


def left_product(high, low, x):
    xh, xl = parts2(x)
    return dot(high, xh) + (dot(high, xl) + dot(low, xh))


def whiten_kernel(alive, starts, halves, x_ref, first_h, first_l, second_h, second_l, third_h, third_l,
                  last_h, last_l, tri_ref, twid_ref, out_ref, sig, pad):
    lane = lax.broadcasted_iota(jnp.int32, (Q, 128), 1)
    sig[...] = jnp.zeros_like(sig)
    pad[...] = jnp.zeros_like(pad)
    normed = []
    for r in range(2):
        gate = alive[r].astype(f32)
        half = halves[r]
        for s in range(2):
            base = (r * 2 + s) * 48
            for h in range(2):
                piece = x_ref[pl.ds(s * 4 + r * 2 + h, 16, stride=8), :]
                sig[pl.ds(base + h, 16, stride=2), :] = piece * gate
            start = starts[s]
            whole = start // 128
            part = start % 128
            here = sig[pl.ds(base + whole, Q), :]
            after = sig[pl.ds(base + whole + 1, Q), :]
            turn = lax.rem(128 - part, 128)
            moved = jnp.where(lane + part < 128, pltpu.roll(here, turn, 1), pltpu.roll(after, turn, 1))
            pad[pl.ds(base + 8, Q), :] = moved
        row = lax.broadcasted_iota(jnp.int32, (128, 128), 0)
        col = lax.broadcasted_iota(jnp.int32, (128, 128), 1)
        gap = row - col
        bands = (gap >= 128 - half, jnp.abs(gap) <= half, -gap >= 128 - half)
        total = None
        signal = jnp.concatenate([pad[pl.ds((r * 2 + s) * 48 + 8, Q), :] for s in range(2)], axis=0)
        for k, band in enumerate(bands):
            weight = jnp.where(band, 1.0, 0.0).astype(bf16)
            value = jnp.concatenate([pad[pl.ds((r * 2 + s) * 48 + 7 + k, Q), :] for s in range(2)], axis=0)
            for term in parts3(jnp.abs(value)):
                add = dot(term, weight)
                total = add if total is None else total + add
        level = total / (2 * half + 1).astype(f32)
        normed.append(signal / (level + TINY))
    x = jnp.concatenate(normed, axis=0)
    cos_t = twid_ref[0:128, :]
    sin_t = twid_ref[128:256, :]
    stage = left_product(first_h[...], first_l[...], x)
    re, im = stage[0:128], stage[128:256]
    turned = jnp.concatenate([re * cos_t + im * sin_t, im * cos_t - re * sin_t], axis=1)
    spec = right_product(turned, second_h[...], second_l[...])
    square = spec * spec
    size = jnp.sqrt(square + pltpu.roll(square, BINS, 1))
    sums = None
    for term in parts3(size):
        add = dot(tri_ref[...], term)
        sums = add if sums is None else sums + add
    smooth = (sums[0:128] + pltpu.roll(sums[128:256], 1, 1) + pltpu.roll(sums[256:384], 127, 1)) / 65.0
    k1 = lax.broadcasted_iota(jnp.int32, (128, 128), 0) % Q
    jj = lax.broadcasted_iota(jnp.int32, (128, 128), 1) % BINS
    bins = k1 + Q * (jj - 1)
    band = (bins >= BAND_LO) & (bins <= BAND_HI)
    gain = jnp.where(band, 2.0 / math.sqrt(NT), 0.0) / (smooth + TINY)
    stage = right_product(spec * gain, third_h[...], third_l[...])
    re, im = stage[:, 0:128], stage[:, 128:256]
    turned = jnp.concatenate([re * cos_t - im * sin_t, im * cos_t + re * sin_t], axis=0)
    white = left_product(last_h[...], last_l[...], turned)
    rolled = pltpu.roll(white, 64, 1)
    for r in range(2):
        sig[pl.ds(r * 40, Q), :] = white[r * 64:r * 64 + Q]
        pad[pl.ds(r * 48 + 8, Q), :] = rolled[r * 64 + Q:r * 64 + 2 * Q]
        pad[pl.ds(r * 48 + 40, 8), :] = jnp.zeros((8, 128), f32)
        pad[pl.ds(r * 48, 8), :] = jnp.zeros((8, 128), f32)
    low = lax.broadcasted_iota(jnp.int32, (2, 128), 1) < 64
    for m in range(Q):
        out_ref[:, m * 128:(m + 1) * 128] = sig[pl.ds(m, 2, stride=40), :].astype(bf16)
    for m in range(Q + 1):
        a = pad[pl.ds(7 + m, 2, stride=48), :]
        b = pad[pl.ds(8 + m, 2, stride=48), :]
        out_ref[:, (Q + m) * 128:(Q + m + 1) * 128] = jnp.where(low, a, b).astype(bf16)


def whiten(x, alive, starts, halves):
    consts = [jnp.asarray(t) for t in tables()]
    smem = pl.BlockSpec(memory_space=pltpu.SMEM)
    vmem = pl.BlockSpec(memory_space=pltpu.VMEM)
    return pl.pallas_call(
        whiten_kernel,
        out_shape=jax.ShapeDtypeStruct((2, LINE), bf16),
        in_specs=[smem] * 3 + [vmem] * (1 + len(consts)),
        out_specs=vmem,
        scratch_shapes=[pltpu.VMEM((4 * 48, 128), f32), pltpu.VMEM((4 * 48, 128), f32)],
        name="whiten",
    )(alive, starts, halves, x, *consts)


def corr_kernel(xi_ref, xj_ref, out_ref, xi, xj, acc, left, right, tall, form):
    for src, dst in ((xi_ref, xi), (xj_ref, xj)):
        dst[:, 128:128 + LINE] = src[...]
        dst[:, 0:128] = src[:, LINE - 128:LINE]
        dst[:, 128 + LINE:256 + LINE] = src[:, 0:128]
    acc[...] = jnp.zeros_like(acc)

    @pl.loop(0, LINE // CHUNK)
    def _(step):
        at = pl.multiple_of(step * CHUNK, 128)
        wide = CHUNK + 256
        line_i = xi[:, pl.ds(at, wide)]
        line_j = xj[:, pl.ds(at, wide)]
        for a in range(A_BLOCKS + 1):
            shift = (STEP * a - LAG) % wide
            moved = pltpu.roll(line_i, shift, 1) if shift else line_i
            left[a * 32:(a + 1) * 32, :] = moved[:, 128:128 + CHUNK]
        for b in range(STEP):
            moved = pltpu.roll(line_j, wide - b, 1) if b else line_j
            right[b * 32:(b + 1) * 32, :] = moved[:, 128:128 + CHUNK]
        acc[...] += lax.dot_general(left[...], right[...], (((1,), (1,)), ((), ())), preferred_element_type=f32)

    scale = 1.0 / math.sqrt(2 * NT)
    for bh in range(4):
        tall[bh * 288:(bh + 1) * 288, :] = acc[:, bh * 128:(bh + 1) * 128] * scale
    form[64:72, :] = jnp.zeros((8, 128), f32)
    for t in range(16):
        for bh in range(4):
            for r in range(2):
                form[bh * 16 + r * 8:bh * 16 + r * 8 + 8, :] = tall[pl.ds(bh * 288 + t * 2 + r, 8, stride=32), :]
        form[64:66, :] = tall[256 + t * 2:258 + t * 2, :]
        out_ref[t] = form[...].astype(bf16)


def correlate(xi, xj):
    vmem = pl.BlockSpec(memory_space=pltpu.VMEM)
    rows = 32 * (A_BLOCKS + 1)
    cols = 32 * STEP
    return pl.pallas_call(
        corr_kernel,
        out_shape=jax.ShapeDtypeStruct((16, 72, 128), bf16),
        in_specs=[vmem] * 2,
        out_specs=vmem,
        scratch_shapes=[
            pltpu.VMEM((32, LINE + 256), bf16), pltpu.VMEM((32, LINE + 256), bf16),
            pltpu.VMEM((rows, cols), f32), pltpu.VMEM((rows, CHUNK), bf16), pltpu.VMEM((cols, CHUNK), bf16),
            pltpu.VMEM((4 * rows, 128), f32), pltpu.VMEM((72, 128), f32),
        ],
        compiler_params=pltpu.CompilerParams(vmem_limit_bytes=48 << 20),
        name="correlate",
    )(xi, xj)


def place_kernel(own, x_ref, perm_ref, out_ref, rows, res):
    lane = lax.broadcasted_iota(jnp.int32, (16, 128), 1) // 32

    def turn(value, by):
        by = by % 128
        return pltpu.roll(value, by, 1) if by else value

    for hi in range(4):
        for bh in range(5):
            source = [x_ref[hi * 4 + lo, bh * 16:bh * 16 + 16, :].astype(f32) if bh < 4 else
                      jnp.concatenate([x_ref[hi * 4 + lo, 64:72, :].astype(f32)] * 2, axis=0) for lo in range(4)]
            for bl in range(4 if bh < 4 else 1):
                value = turn(source[0], -32 * bl)
                for lo in range(1, 4):
                    value = jnp.where(lane == lo, turn(source[lo], 32 * (lo - bl)), value)
                at = (bh * 4 + bl) * 16
                rows[at:at + 16, hi * 128:(hi + 1) * 128] = value.astype(bf16)
    moved = dot(rows[...], perm_ref[...])
    row = lax.broadcasted_iota(jnp.int32, moved.shape, 0)
    col = lax.broadcasted_iota(jnp.int32, moved.shape, 1)
    which = jnp.where(row < 256, (row // 8) % 2, row % 2)
    moved = jnp.where(col == own[0] + which, 0.0, moved)
    for hi in range(4):
        span = slice(hi * 128, (hi + 1) * 128)
        res[hi * 272:(hi + 1) * 272, :] = moved[:, span]
        for b in range(16):
            for a in range(8):
                out_ref[16 * a + b, :, span] = res[pl.ds(hi * 272 + b * 16 + a, 2, stride=8), :].astype(bf16)
        out_ref[128, :, span] = res[hi * 272 + 256:hi * 272 + 258, :].astype(bf16)


def place(own, x, perm):
    smem = pl.BlockSpec(memory_space=pltpu.SMEM)
    vmem = pl.BlockSpec(memory_space=pltpu.VMEM)
    return pl.pallas_call(
        place_kernel,
        out_shape=jax.ShapeDtypeStruct((129, 2, 512), bf16),
        in_specs=[smem, vmem, vmem],
        out_specs=vmem,
        scratch_shapes=[pltpu.VMEM((272, 512), bf16), pltpu.VMEM((4 * 272, 128), f32)],
        name="place",
    )(own, x, perm)


def on_device(raw, alive, seg_start, norm_half):
    chan_index = lax.axis_index("chan")
    time_index = lax.axis_index("tm")
    sent = raw.reshape(2, 16, 2, 2, 128).transpose(1, 0, 2, 3, 4).reshape(16, 8, 128)
    traces = lax.all_to_all(sent, "tm", split_axis=0, concat_axis=0, tiled=True).reshape(128, 128)
    white = whiten(traces, alive, seg_start, norm_half)
    spread = jnp.broadcast_to(white[None], (16, 2, LINE))
    rows = lax.all_to_all(spread, "tm", split_axis=0, concat_axis=0, tiled=True).reshape(32, LINE)
    cols = lax.all_gather(white, "chan", axis=0, tiled=True)
    block = correlate(rows, cols)
    back = lax.all_to_all(block, "tm", split_axis=0, concat_axis=0, tiled=True)
    lanes = jnp.arange(512, dtype=jnp.int32)
    holder = lanes // 32
    group = (lanes % 32) // 2
    target = group * 32 + holder * 2 + lanes % 2
    perm = (target[:, None] == lanes[None, :]).astype(bf16)
    own = ((chan_index * 16 + time_index) * 2).astype(jnp.int32).reshape(1)
    return place(own, back, perm).transpose(1, 0, 2)


def solution(mesh):
    return jax.shard_map(
        on_device,
        mesh=mesh,
        in_specs=(P(None, "chan", "tm"), P(("chan", "tm")), P(), P(("chan", "tm"))),
        out_specs=P(("chan", "tm"), None, None),
        check_vma=False,
    )
```

```python
import functools
import math

import jax
import jax.numpy as jnp
import ml_dtypes
import numpy as np
from jax import lax
from jax.experimental import pallas as pl
from jax.experimental.pallas import tpu as pltpu
from jax.sharding import Mesh, PartitionSpec as P

LAG = 64
TINY = 1e-05
NT = 4096
Q = 32
GROUPS = 4
LINE = 2 * (NT + LAG)
STEP = 16
A_BLOCKS = 2 * LAG // STEP
CHUNK = 13 * 128
BAND_LO = 16
BAND_HI = 1638
BINS = 64

bf16 = jnp.bfloat16
f32 = jnp.float32


def split_const(table):
    high = table.astype(ml_dtypes.bfloat16)
    low = (table - high.astype(np.float64)).astype(ml_dtypes.bfloat16)
    return high, low


@functools.lru_cache(maxsize=None)
def tables():
    q = np.arange(Q)
    p = np.arange(128)
    eye = np.eye(GROUPS)
    ang_q = 2 * np.pi * np.outer(q, q) / Q
    cos_q, sin_q = np.kron(eye, np.cos(ang_q)), np.kron(eye, np.sin(ang_q))
    first = np.concatenate([cos_q, -sin_q], axis=0)
    last = np.concatenate([cos_q, -sin_q], axis=1)
    ang_t = 2 * np.pi * np.outer(q, p) / NT
    twiddle = np.concatenate([np.tile(np.cos(ang_t), (GROUPS, 1)), np.tile(np.sin(ang_t), (GROUPS, 1))], axis=0)
    ang_p = 2 * np.pi * np.outer(p, np.arange(BINS) - 1) / 128
    cos_p, sin_p = np.cos(ang_p), np.sin(ang_p)
    second = np.block([[cos_p, -sin_p], [sin_p, cos_p]])
    third = np.block([[cos_p.T, sin_p.T], [-sin_p.T, cos_p.T]])
    tri = np.concatenate([
        np.kron(eye, np.ones((Q, Q))),
        np.kron(eye, (q[None, :] >= q[:, None]).astype(float)),
        np.kron(eye, (q[None, :] <= q[:, None]).astype(float)),
    ], axis=0)
    out = []
    for table in (first, second, third, last):
        out.extend(split_const(table))
    out.append(tri.astype(ml_dtypes.bfloat16))
    out.append(twiddle.astype(np.float32))
    return out


def parts2(x):
    high = x.astype(bf16)
    return high, (x - high.astype(f32)).astype(bf16)


def parts3(x):
    high = x.astype(bf16)
    rest = x - high.astype(f32)
    mid = rest.astype(bf16)
    return high, mid, (rest - mid.astype(f32)).astype(bf16)


def dot(a, b):
    return jnp.dot(a, b, preferred_element_type=f32)


def right_product(x, high, low):
    xh, xl = parts2(x)
    return dot(xh, high) + (dot(xl, high) + dot(xh, low))


def left_product(high, low, x):
    xh, xl = parts2(x)
    return dot(high, xh) + (dot(high, xl) + dot(low, xh))


def whiten_kernel(alive, starts, halves, x_ref, first_h, first_l, second_h, second_l, third_h, third_l,
                  last_h, last_l, tri_ref, twid_ref, out_ref, spread_ref, sig, pad):
    lane = lax.broadcasted_iota(jnp.int32, (Q, 128), 1)
    sig[...] = jnp.zeros_like(sig)
    pad[...] = jnp.zeros_like(pad)
    normed = []
    for r in range(2):
        gate = alive[r].astype(f32)
        half = halves[r]
        for s in range(2):
            base = (r * 2 + s) * 48
            for h in range(2):
                piece = x_ref[pl.ds(s * 4 + r * 2 + h, 16, stride=8), :]
                sig[pl.ds(base + h, 16, stride=2), :] = piece * gate
            start = starts[s]
            whole = start // 128
            part = start % 128
            here = sig[pl.ds(base + whole, Q), :]
            after = sig[pl.ds(base + whole + 1, Q), :]
            turn = lax.rem(128 - part, 128)
            moved = jnp.where(lane + part < 128, pltpu.roll(here, turn, 1), pltpu.roll(after, turn, 1))
            pad[pl.ds(base + 8, Q), :] = moved
        row = lax.broadcasted_iota(jnp.int32, (128, 128), 0)
        col = lax.broadcasted_iota(jnp.int32, (128, 128), 1)
        gap = row - col
        bands = (gap >= 128 - half, jnp.abs(gap) <= half, -gap >= 128 - half)
        total = None
        signal = jnp.concatenate([pad[pl.ds((r * 2 + s) * 48 + 8, Q), :] for s in range(2)], axis=0)
        for k, band in enumerate(bands):
            weight = jnp.where(band, 1.0, 0.0).astype(bf16)
            value = jnp.concatenate([pad[pl.ds((r * 2 + s) * 48 + 7 + k, Q), :] for s in range(2)], axis=0)
            for term in parts3(jnp.abs(value)):
                add = dot(term, weight)
                total = add if total is None else total + add
        level = total / (2 * half + 1).astype(f32)
        normed.append(signal / (level + TINY))
    x = jnp.concatenate(normed, axis=0)
    cos_t = twid_ref[0:128, :]
    sin_t = twid_ref[128:256, :]
    stage = left_product(first_h[...], first_l[...], x)
    re, im = stage[0:128], stage[128:256]
    turned = jnp.concatenate([re * cos_t + im * sin_t, im * cos_t - re * sin_t], axis=1)
    spec = right_product(turned, second_h[...], second_l[...])
    square = spec * spec
    size = jnp.sqrt(square + pltpu.roll(square, BINS, 1))
    sums = None
    for term in parts3(size):
        add = dot(tri_ref[...], term)
        sums = add if sums is None else sums + add
    smooth = (sums[0:128] + pltpu.roll(sums[128:256], 1, 1) + pltpu.roll(sums[256:384], 127, 1)) / 65.0
    k1 = lax.broadcasted_iota(jnp.int32, (128, 128), 0) % Q
    jj = lax.broadcasted_iota(jnp.int32, (128, 128), 1) % BINS
    bins = k1 + Q * (jj - 1)
    band = (bins >= BAND_LO) & (bins <= BAND_HI)
    gain = jnp.where(band, 2.0 / math.sqrt(NT), 0.0) / (smooth + TINY)
    stage = right_product(spec * gain, third_h[...], third_l[...])
    re, im = stage[:, 0:128], stage[:, 128:256]
    turned = jnp.concatenate([re * cos_t - im * sin_t, im * cos_t + re * sin_t], axis=0)
    white = left_product(last_h[...], last_l[...], turned)
    rolled = pltpu.roll(white, 64, 1)
    for r in range(2):
        sig[pl.ds(r * 40, Q), :] = white[r * 64:r * 64 + Q]
        pad[pl.ds(r * 48 + 8, Q), :] = rolled[r * 64 + Q:r * 64 + 2 * Q]
        pad[pl.ds(r * 48 + 40, 8), :] = jnp.zeros((8, 128), f32)
        pad[pl.ds(r * 48, 8), :] = jnp.zeros((8, 128), f32)
    low = lax.broadcasted_iota(jnp.int32, (2, 128), 1) < 64
    for m in range(2 * Q + 1):
        if m < Q:
            value = sig[pl.ds(m, 2, stride=40), :]
        else:
            value = jnp.where(low, pad[pl.ds(7 + m - Q, 2, stride=48), :], pad[pl.ds(8 + m - Q, 2, stride=48), :])
        value = value.astype(bf16)
        out_ref[:, m * 128:(m + 1) * 128] = value
        for e in range(16):
            spread_ref[e, :, m * 128:(m + 1) * 128] = value


def whiten(x, alive, starts, halves):
    consts = [jnp.asarray(t) for t in tables()]
    smem = pl.BlockSpec(memory_space=pltpu.SMEM)
    vmem = pl.BlockSpec(memory_space=pltpu.VMEM)
    return pl.pallas_call(
        whiten_kernel,
        out_shape=(jax.ShapeDtypeStruct((2, LINE), bf16), jax.ShapeDtypeStruct((16, 2, LINE), bf16)),
        in_specs=[smem] * 3 + [vmem] * (1 + len(consts)),
        out_specs=(vmem, vmem),
        scratch_shapes=[pltpu.VMEM((4 * 48, 128), f32), pltpu.VMEM((4 * 48, 128), f32)],
        name="whiten",
    )(alive, starts, halves, x, *consts)


def load_lines(refs, line):
    at = 0
    for ref in refs:
        for k in range(ref.shape[0]):
            line[at:at + 2, 128:128 + LINE] = ref[k]
            at += 2
    line[:, 0:128] = line[:, LINE:LINE + 128]
    line[:, 128 + LINE:256 + LINE] = line[:, 128:256]


def corr_kernel(rows_ref, *rest):
    cols, (out_ref, xi, xj, acc, left, right, tall, form) = rest[:-8], rest[-8:]
    load_lines([rows_ref], xi)
    load_lines(cols, xj)
    acc[...] = jnp.zeros_like(acc)

    @pl.loop(0, LINE // CHUNK)
    def _(step):
        at = pl.multiple_of(step * CHUNK, 128)
        wide = CHUNK + 256
        line_i = xi[:, pl.ds(at, wide)]
        line_j = xj[:, pl.ds(at, wide)]
        for a in range(A_BLOCKS + 1):
            shift = (STEP * a - LAG) % wide
            moved = pltpu.roll(line_i, shift, 1) if shift else line_i
            left[a * 32:(a + 1) * 32, :] = moved[:, 128:128 + CHUNK]
        for b in range(STEP):
            moved = pltpu.roll(line_j, wide - b, 1) if b else line_j
            right[b * 32:(b + 1) * 32, :] = moved[:, 128:128 + CHUNK]
        acc[...] += lax.dot_general(left[...], right[...], (((1,), (1,)), ((), ())), preferred_element_type=f32)

    scale = 1.0 / math.sqrt(2 * NT)
    for bh in range(4):
        tall[bh * 288:(bh + 1) * 288, :] = acc[:, bh * 128:(bh + 1) * 128] * scale
    form[64:72, :] = jnp.zeros((8, 128), f32)
    for t in range(16):
        for bh in range(4):
            for r in range(2):
                form[bh * 16 + r * 8:bh * 16 + r * 8 + 8, :] = tall[pl.ds(bh * 288 + t * 2 + r, 8, stride=32), :]
        form[64:66, :] = tall[256 + t * 2:258 + t * 2, :]
        out_ref[t] = form[...].astype(bf16)


def correlate(rows_in, cols_in):
    vmem = pl.BlockSpec(memory_space=pltpu.VMEM)
    rows = 32 * (A_BLOCKS + 1)
    cols = 32 * STEP
    return pl.pallas_call(
        corr_kernel,
        out_shape=jax.ShapeDtypeStruct((16, 72, 128), bf16),
        in_specs=[vmem] * (1 + len(cols_in)),
        out_specs=vmem,
        scratch_shapes=[
            pltpu.VMEM((32, LINE + 256), bf16), pltpu.VMEM((32, LINE + 256), bf16),
            pltpu.VMEM((rows, cols), f32), pltpu.VMEM((rows, CHUNK), bf16), pltpu.VMEM((cols, CHUNK), bf16),
            pltpu.VMEM((4 * rows, 128), f32), pltpu.VMEM((72, 128), f32),
        ],
        compiler_params=pltpu.CompilerParams(vmem_limit_bytes=32 << 20),
        cost_estimate=pl.CostEstimate(flops=2 * rows * cols * LINE, bytes_accessed=4 << 20, transcendentals=0),
        name="correlate",
    )(rows_in, *cols_in)


def place_kernel(own, x_ref, perm_ref, out_ref, rows, res):
    lane = lax.broadcasted_iota(jnp.int32, (16, 128), 1) // 32

    def turn(value, by):
        by = by % 128
        return pltpu.roll(value, by, 1) if by else value

    for hi in range(4):
        for bh in range(5):
            source = [x_ref[hi * 4 + lo, bh * 16:bh * 16 + 16, :].astype(f32) if bh < 4 else
                      jnp.concatenate([x_ref[hi * 4 + lo, 64:72, :].astype(f32)] * 2, axis=0) for lo in range(4)]
            for bl in range(4 if bh < 4 else 1):
                value = turn(source[0], -32 * bl)
                for lo in range(1, 4):
                    value = jnp.where(lane == lo, turn(source[lo], 32 * (lo - bl)), value)
                at = (bh * 4 + bl) * 16
                rows[at:at + 16, hi * 128:(hi + 1) * 128] = value.astype(bf16)
    moved = dot(rows[...], perm_ref[...])
    row = lax.broadcasted_iota(jnp.int32, moved.shape, 0)
    col = lax.broadcasted_iota(jnp.int32, moved.shape, 1)
    which = jnp.where(row < 256, (row // 8) % 2, row % 2)
    moved = jnp.where(col == own[0] + which, 0.0, moved)
    for hi in range(4):
        span = slice(hi * 128, (hi + 1) * 128)
        res[hi * 272:(hi + 1) * 272, :] = moved[:, span]
        for b in range(16):
            for a in range(8):
                out_ref[16 * a + b, :, span] = res[pl.ds(hi * 272 + b * 16 + a, 2, stride=8), :].astype(bf16)
        out_ref[128, :, span] = res[hi * 272 + 256:hi * 272 + 258, :].astype(bf16)


def place(own, x, perm):
    smem = pl.BlockSpec(memory_space=pltpu.SMEM)
    vmem = pl.BlockSpec(memory_space=pltpu.VMEM)
    return pl.pallas_call(
        place_kernel,
        out_shape=jax.ShapeDtypeStruct((129, 2, 512), bf16),
        in_specs=[smem, vmem, vmem],
        out_specs=vmem,
        scratch_shapes=[pltpu.VMEM((272, 512), bf16), pltpu.VMEM((4 * 272, 128), f32)],
        compiler_params=pltpu.CompilerParams(vmem_limit_bytes=16 << 20),
        name="place",
    )(own, x, perm)


PLANE = ("yl", "x", "yh")
SLABS = ("x", "yh", "core")


def passed(value, axis, by):
    length = lax.axis_size(axis)
    return lax.ppermute(value, axis, [(i, (i + by) % length) for i in range(length)])


def on_device(raw, alive, seg_start, norm_half):
    z, yl, x, yh, core = (lax.axis_index(axis) for axis in ("z", "yl", "x", "yh", "core"))
    sent = raw.reshape(2, 16, 2, 2, 128).transpose(1, 0, 2, 3, 4).reshape(16, 8, 128)
    traces = lax.all_to_all(sent, SLABS, split_axis=0, concat_axis=0, tiled=True).reshape(128, 128)
    white, spread = whiten(traces, alive, seg_start, norm_half)
    rows = lax.all_to_all(spread, PLANE, split_axis=0, concat_axis=0, tiled=True)
    white = white[None]
    up, down = passed(white, "z", 1), passed(white, "z", -1)
    near = jnp.concatenate([white, up, down], axis=0)
    far_up = passed(near, "z", 3)
    far_down = passed(jnp.concatenate([white, up], axis=0), "z", -3)
    near_other = passed(near, "core", 1)
    far_other = passed(jnp.concatenate([far_up, far_down], axis=0), "core", 1)
    block = correlate(rows, [near, far_up, far_down, near_other, far_other])
    back = lax.all_to_all(block, PLANE, split_axis=0, concat_axis=0, tiled=True)
    k = np.arange(512)
    e, half, j = k // 32, (k // 16) % 2, k % 16
    offset = np.repeat([0, 7, 1, 5, 4, 6, 3, 2], 2)[j]
    fixed = (e // 8) * 32 + ((e // 2) % 4) * 8 + (e % 2) * 4 + j % 2
    from_z = (z + jnp.asarray(offset, jnp.int32)) & 7
    target = from_z * 64 + jnp.asarray(fixed, jnp.int32) + (core ^ jnp.asarray(half, jnp.int32)) * 2
    k = lax.iota(jnp.int32, 512)
    perm = (target[:, None] == k[None, :]).astype(bf16)
    own = (((z * 2 + yl) * 16 + x * 4 + yh * 2 + core) * 2).astype(jnp.int32).reshape(1)
    return place(own, back, perm).transpose(1, 0, 2)


def solution(mesh):
    fine = Mesh(mesh.devices.reshape(8, 2, 4, 2, 2), ("z", "yl", "x", "yh", "core"))
    both = ("z", "yl", "x", "yh", "core")
    return jax.shard_map(
        on_device,
        mesh=fine,
        in_specs=(P(None, ("z", "yl"), SLABS), P(both), P(), P(both)),
        out_specs=P(both, None, None),
        check_vma=False,
    )
```

```python
import functools
import math

import jax
import jax.numpy as jnp
import ml_dtypes
import numpy as np
from jax import lax
from jax.experimental import pallas as pl
from jax.experimental.pallas import tpu as pltpu
from jax.sharding import Mesh, PartitionSpec as P

LAG = 64
TINY = 1e-05
NT = 4096
Q = 32
GROUPS = 4
LINE = 2 * (NT + LAG)
STEP = 16
A_BLOCKS = 2 * LAG // STEP
CHUNK = 13 * 128
BAND_LO = 16
BAND_HI = 1638
BINS = 64

bf16 = jnp.bfloat16
f32 = jnp.float32


def split_const(table):
    high = table.astype(ml_dtypes.bfloat16)
    low = (table - high.astype(np.float64)).astype(ml_dtypes.bfloat16)
    return high, low


@functools.lru_cache(maxsize=None)
def tables():
    q = np.arange(Q)
    p = np.arange(128)
    eye = np.eye(GROUPS)
    ang_q = 2 * np.pi * np.outer(q, q) / Q
    cos_q, sin_q = np.kron(eye, np.cos(ang_q)), np.kron(eye, np.sin(ang_q))
    first = np.concatenate([cos_q, -sin_q], axis=0)
    last = np.concatenate([cos_q, -sin_q], axis=1)
    ang_t = 2 * np.pi * np.outer(q, p) / NT
    twiddle = np.concatenate([np.tile(np.cos(ang_t), (GROUPS, 1)), np.tile(np.sin(ang_t), (GROUPS, 1))], axis=0)
    ang_p = 2 * np.pi * np.outer(p, np.arange(BINS) - 1) / 128
    cos_p, sin_p = np.cos(ang_p), np.sin(ang_p)
    second = np.block([[cos_p, -sin_p], [sin_p, cos_p]])
    third = np.block([[cos_p.T, sin_p.T], [-sin_p.T, cos_p.T]])
    tri = np.concatenate([
        np.kron(eye, np.ones((Q, Q))),
        np.kron(eye, (q[None, :] >= q[:, None]).astype(float)),
        np.kron(eye, (q[None, :] <= q[:, None]).astype(float)),
    ], axis=0)
    out = []
    for table in (first, second, third, last):
        for piece in split_const(table):
            out.extend(piece[:, at:at + 128] for at in range(0, piece.shape[1], 128))
    out.append(tri.astype(ml_dtypes.bfloat16))
    return [np.concatenate(out, axis=0), twiddle.astype(np.float32)]


def parts2(x):
    high = x.astype(bf16)
    return high, (x - high.astype(f32)).astype(bf16)


def parts3(x):
    high = x.astype(bf16)
    rest = x - high.astype(f32)
    mid = rest.astype(bf16)
    return high, mid, (rest - mid.astype(f32)).astype(bf16)


def dot(a, b):
    return jnp.dot(a, b, preferred_element_type=f32)


def right_product(x, high, low):
    xh, xl = parts2(x)
    return dot(xh, high) + (dot(xl, high) + dot(xh, low))


def left_product(high, low, x):
    xh, xl = parts2(x)
    return dot(high, xh) + (dot(high, xl) + dot(low, xh))


def whiten_kernel(alive, starts, halves, x_ref, mats, twid_ref, out_ref, spread_ref, sig, pad):
    lane = lax.broadcasted_iota(jnp.int32, (Q, 128), 1)
    sig[...] = jnp.zeros_like(sig)
    pad[...] = jnp.zeros_like(pad)
    normed = []
    for r in range(2):
        gate = alive[r].astype(f32)
        half = halves[r]
        for s in range(2):
            base = (r * 2 + s) * 48
            for h in range(2):
                piece = x_ref[pl.ds(s * 4 + r * 2 + h, 16, stride=8), :]
                sig[pl.ds(base + h, 16, stride=2), :] = piece * gate
            start = starts[s]
            whole = start // 128
            part = start % 128
            here = sig[pl.ds(base + whole, Q), :]
            after = sig[pl.ds(base + whole + 1, Q), :]
            turn = lax.rem(128 - part, 128)
            moved = jnp.where(lane + part < 128, pltpu.roll(here, turn, 1), pltpu.roll(after, turn, 1))
            pad[pl.ds(base + 8, Q), :] = moved
        row = lax.broadcasted_iota(jnp.int32, (128, 128), 0)
        col = lax.broadcasted_iota(jnp.int32, (128, 128), 1)
        gap = row - col
        bands = (gap >= 128 - half, jnp.abs(gap) <= half, -gap >= 128 - half)
        total = None
        signal = jnp.concatenate([pad[pl.ds((r * 2 + s) * 48 + 8, Q), :] for s in range(2)], axis=0)
        for k, band in enumerate(bands):
            weight = jnp.where(band, 1.0, 0.0).astype(bf16)
            value = jnp.concatenate([pad[pl.ds((r * 2 + s) * 48 + 7 + k, Q), :] for s in range(2)], axis=0)
            for term in parts3(jnp.abs(value)):
                add = dot(term, weight)
                total = add if total is None else total + add
        level = total / (2 * half + 1).astype(f32)
        normed.append(signal / (level + TINY))
    x = jnp.concatenate(normed, axis=0)
    first_h, first_l, second_h, second_l = (mats[k * 256:(k + 1) * 256, :] for k in range(4))
    third_h, third_l, last_h, last_l = (
        jnp.concatenate([mats[k * 256:k * 256 + 128, :], mats[k * 256 + 128:(k + 1) * 256, :]], axis=1)
        for k in range(4, 8))
    cos_t = twid_ref[0:128, :]
    sin_t = twid_ref[128:256, :]
    stage = left_product(first_h, first_l, x)
    re, im = stage[0:128], stage[128:256]
    turned = jnp.concatenate([re * cos_t + im * sin_t, im * cos_t - re * sin_t], axis=1)
    spec = right_product(turned, second_h, second_l)
    square = spec * spec
    size = jnp.sqrt(square + pltpu.roll(square, BINS, 1))
    sums = None
    for term in parts3(size):
        add = dot(mats[2048:2432, :], term)
        sums = add if sums is None else sums + add
    smooth = (sums[0:128] + pltpu.roll(sums[128:256], 1, 1) + pltpu.roll(sums[256:384], 127, 1)) / 65.0
    k1 = lax.broadcasted_iota(jnp.int32, (128, 128), 0) % Q
    jj = lax.broadcasted_iota(jnp.int32, (128, 128), 1) % BINS
    bins = k1 + Q * (jj - 1)
    band = (bins >= BAND_LO) & (bins <= BAND_HI)
    gain = jnp.where(band, 2.0 / math.sqrt(NT), 0.0) / (smooth + TINY)
    stage = right_product(spec * gain, third_h, third_l)
    re, im = stage[:, 0:128], stage[:, 128:256]
    turned = jnp.concatenate([re * cos_t - im * sin_t, im * cos_t + re * sin_t], axis=0)
    white = left_product(last_h, last_l, turned)
    rolled = pltpu.roll(white, 64, 1)
    for r in range(2):
        sig[pl.ds(r * 40, Q), :] = white[r * 64:r * 64 + Q]
        pad[pl.ds(r * 48 + 8, Q), :] = rolled[r * 64 + Q:r * 64 + 2 * Q]
        pad[pl.ds(r * 48 + 40, 8), :] = jnp.zeros((8, 128), f32)
        pad[pl.ds(r * 48, 8), :] = jnp.zeros((8, 128), f32)
    low = lax.broadcasted_iota(jnp.int32, (2, 128), 1) < 64
    for m in range(2 * Q + 1):
        if m < Q:
            value = sig[pl.ds(m, 2, stride=40), :]
        else:
            value = jnp.where(low, pad[pl.ds(7 + m - Q, 2, stride=48), :], pad[pl.ds(8 + m - Q, 2, stride=48), :])
        value = value.astype(bf16)
        out_ref[:, m * 128:(m + 1) * 128] = value
        for e in range(16):
            spread_ref[e, :, m * 128:(m + 1) * 128] = value


def whiten(x, alive, starts, halves):
    consts = [jnp.asarray(t) for t in tables()]
    smem = pl.BlockSpec(memory_space=pltpu.SMEM)
    vmem = pl.BlockSpec(memory_space=pltpu.VMEM)
    return pl.pallas_call(
        whiten_kernel,
        out_shape=(jax.ShapeDtypeStruct((2, LINE), bf16), jax.ShapeDtypeStruct((16, 2, LINE), bf16)),
        in_specs=[smem] * 3 + [vmem] * 3,
        out_specs=(vmem, vmem),
        scratch_shapes=[pltpu.VMEM((4 * 48, 128), f32), pltpu.VMEM((4 * 48, 128), f32)],
        name="whiten",
    )(alive, starts, halves, x, *consts)


def load_lines(refs, line):
    at = 0
    for ref in refs:
        for k in range(ref.shape[0]):
            line[at:at + 2, 128:128 + LINE] = ref[k]
            at += 2
    line[:, 0:128] = line[:, LINE:LINE + 128]
    line[:, 128 + LINE:256 + LINE] = line[:, 128:256]


def corr_kernel(rows_ref, *rest):
    cols, (out_ref, held, sems, xi, xj, acc, left0, right0, left1, right1, tall, form) = rest[:-12], rest[-12:]
    copies, at = [], 0
    for k, ref in enumerate(cols):
        copies.append(pltpu.make_async_copy(ref, held.at[at:at + ref.shape[0]], sems.at[k]))
        copies[-1].start()
        at += ref.shape[0]
    load_lines([rows_ref], xi)
    for copy in copies:
        copy.wait()
    load_lines([held], xj)
    wide = CHUNK + 256
    slots = ((left0, right0), (left1, right1))

    def expand(step):
        left, right = slots[step % 2]
        line_i = xi[:, step * CHUNK:step * CHUNK + wide]
        line_j = xj[:, step * CHUNK:step * CHUNK + wide]
        for a in range(A_BLOCKS + 1):
            shift = (STEP * a - LAG) % wide
            moved = pltpu.roll(line_i, shift, 1) if shift else line_i
            left[a * 32:(a + 1) * 32, :] = moved[:, 128:128 + CHUNK]
        for b in range(STEP):
            moved = pltpu.roll(line_j, wide - b, 1) if b else line_j
            right[b * 32:(b + 1) * 32, :] = moved[:, 128:128 + CHUNK]

    expand(0)
    for step in range(LINE // CHUNK):
        if step + 1 < LINE // CHUNK:
            expand(step + 1)
        left, right = slots[step % 2]
        add = lax.dot_general(left[...], right[...], (((1,), (1,)), ((), ())), preferred_element_type=f32)
        acc[...] = add if step == 0 else acc[...] + add

    scale = 1.0 / math.sqrt(2 * NT)
    for bh in range(4):
        tall[bh * 288:(bh + 1) * 288, :] = acc[:, bh * 128:(bh + 1) * 128] * scale
    form[64:72, :] = jnp.zeros((8, 128), f32)
    for t in range(16):
        for bh in range(4):
            for r in range(2):
                form[bh * 16 + r * 8:bh * 16 + r * 8 + 8, :] = tall[pl.ds(bh * 288 + t * 2 + r, 8, stride=32), :]
        form[64:66, :] = tall[256 + t * 2:258 + t * 2, :]
        out_ref[t] = form[...].astype(bf16)


def correlate(rows_in, cols_in):
    vmem = pl.BlockSpec(memory_space=pltpu.VMEM)
    rows = 32 * (A_BLOCKS + 1)
    cols = 32 * STEP
    return pl.pallas_call(
        corr_kernel,
        out_shape=jax.ShapeDtypeStruct((16, 72, 128), bf16),
        in_specs=[vmem] + [pl.BlockSpec(memory_space=pl.ANY)] * len(cols_in),
        out_specs=vmem,
        scratch_shapes=[
            pltpu.VMEM((16, 2, LINE), bf16), pltpu.SemaphoreType.DMA((len(cols_in),)),
            pltpu.VMEM((32, LINE + 256), bf16), pltpu.VMEM((32, LINE + 256), bf16),
            pltpu.VMEM((rows, cols), f32), pltpu.VMEM((rows, CHUNK), bf16), pltpu.VMEM((cols, CHUNK), bf16),
            pltpu.VMEM((rows, CHUNK), bf16), pltpu.VMEM((cols, CHUNK), bf16),
            pltpu.VMEM((4 * rows, 128), f32), pltpu.VMEM((72, 128), f32),
        ],
        compiler_params=pltpu.CompilerParams(vmem_limit_bytes=32 << 20),
        cost_estimate=pl.CostEstimate(flops=2 * rows * cols * LINE, bytes_accessed=4 << 20, transcendentals=0),
        name="correlate",
    )(rows_in, *cols_in)


def place_kernel(own, x_ref, perm_ref, out_ref, rows, res):
    lane = lax.broadcasted_iota(jnp.int32, (16, 128), 1) // 32

    def turn(value, by):
        by = by % 128
        return pltpu.roll(value, by, 1) if by else value

    for hi in range(4):
        for bh in range(5):
            source = [x_ref[hi * 4 + lo, bh * 16:bh * 16 + 16, :].astype(f32) if bh < 4 else
                      jnp.concatenate([x_ref[hi * 4 + lo, 64:72, :].astype(f32)] * 2, axis=0) for lo in range(4)]
            for bl in range(4 if bh < 4 else 1):
                value = turn(source[0], -32 * bl)
                for lo in range(1, 4):
                    value = jnp.where(lane == lo, turn(source[lo], 32 * (lo - bl)), value)
                at = (bh * 4 + bl) * 16
                rows[at:at + 16, hi * 128:(hi + 1) * 128] = value.astype(bf16)
    moved = dot(rows[...], perm_ref[...])
    row = lax.broadcasted_iota(jnp.int32, moved.shape, 0)
    col = lax.broadcasted_iota(jnp.int32, moved.shape, 1)
    which = jnp.where(row < 256, (row // 8) % 2, row % 2)
    moved = jnp.where(col == own[0] + which, 0.0, moved)
    for hi in range(4):
        span = slice(hi * 128, (hi + 1) * 128)
        res[hi * 272:(hi + 1) * 272, :] = moved[:, span]
        for b in range(16):
            for a in range(8):
                out_ref[16 * a + b, :, span] = res[pl.ds(hi * 272 + b * 16 + a, 2, stride=8), :].astype(bf16)
        out_ref[128, :, span] = res[hi * 272 + 256:hi * 272 + 258, :].astype(bf16)


def place(own, x, perm):
    smem = pl.BlockSpec(memory_space=pltpu.SMEM)
    vmem = pl.BlockSpec(memory_space=pltpu.VMEM)
    return pl.pallas_call(
        place_kernel,
        out_shape=jax.ShapeDtypeStruct((129, 2, 512), bf16),
        in_specs=[smem, vmem, vmem],
        out_specs=vmem,
        scratch_shapes=[pltpu.VMEM((272, 512), bf16), pltpu.VMEM((4 * 272, 128), f32)],
        compiler_params=pltpu.CompilerParams(vmem_limit_bytes=16 << 20),
        name="place",
    )(own, x, perm)


PLANE = ("yl", "x", "yh")
SLABS = ("x", "yh", "core")


def crossed(value):
    return lax.ppermute(value, "core", [(0, 1), (1, 0)])


def shed(value, by):
    pairs = []
    for z in range(8):
        pairs.append((z * 2, (z + by) % 8 * 2))
        pairs.append((z * 2 + 1, (z - by) % 8 * 2 + 1))
    return lax.ppermute(value, ("z", "core"), pairs)


def columns_by_hops(pair):
    one = shed(pair, 1)
    more = shed(jnp.concatenate([pair, one], axis=0), 2)
    four = shed(more[2:4], 1)
    return one, more, four, crossed(one), crossed(more)


def on_device(raw, alive, seg_start, norm_half):
    z, yl, x, yh, core = (lax.axis_index(axis) for axis in ("z", "yl", "x", "yh", "core"))
    sent = raw.reshape(2, 16, 2, 2, 128).transpose(1, 0, 2, 3, 4).reshape(16, 8, 128)
    traces = lax.all_to_all(sent, SLABS, split_axis=0, concat_axis=0, tiled=True).reshape(128, 128)
    white, spread = whiten(traces, alive, seg_start, norm_half)
    rows = lax.all_to_all(spread, PLANE, split_axis=0, concat_axis=0, tiled=True)
    white = white[None]
    pair = jnp.concatenate([white, crossed(white)], axis=0)
    block = correlate(rows, (pair,) + columns_by_hops(pair))
    back = lax.all_to_all(block, PLANE, split_axis=0, concat_axis=0, tiled=True)
    k = np.arange(512)
    e, pair_id, side = k // 32, (k // 4) % 8, (k // 2) % 2
    step = np.array([0, 1, 2, 3, 4, -1, -2, -3])[pair_id]
    side = side ^ (pair_id >= 5)
    fixed = (e // 8) * 32 + ((e // 2) % 4) * 8 + (e % 2) * 4 + k % 2
    from_z = (z + jnp.asarray(step, jnp.int32) * (2 * core - 1)) & 7
    target = from_z * 64 + jnp.asarray(fixed, jnp.int32) + (core ^ jnp.asarray(side, jnp.int32)) * 2
    k = lax.iota(jnp.int32, 512)
    perm = (target[:, None] == k[None, :]).astype(bf16)
    own = (((z * 2 + yl) * 16 + x * 4 + yh * 2 + core) * 2).astype(jnp.int32).reshape(1)
    return place(own, back, perm).transpose(1, 0, 2)


def solution(mesh):
    fine = Mesh(mesh.devices.reshape(8, 2, 4, 2, 2), ("z", "yl", "x", "yh", "core"))
    both = ("z", "yl", "x", "yh", "core")
    return jax.shard_map(
        on_device,
        mesh=fine,
        in_specs=(P(None, ("z", "yl"), SLABS), P(both), P(), P(both)),
        out_specs=P(both, None, None),
        check_vma=False,
    )
```

```python
import functools
import math

import jax
import jax.numpy as jnp
import ml_dtypes
import numpy as np
from jax import lax
from jax.experimental import pallas as pl
from jax.experimental.pallas import tpu as pltpu
from jax.sharding import Mesh, PartitionSpec as P

LAG = 64
TINY = 1e-05
NT = 4096
Q = 32
GROUPS = 4
LINE = 2 * (NT + LAG)
STEP = 16
A_BLOCKS = 2 * LAG // STEP
CHUNK = 13 * 128
BAND_LO = 16
BAND_HI = 1638
BINS = 64

bf16 = jnp.bfloat16
f32 = jnp.float32


def split_const(table):
    high = table.astype(ml_dtypes.bfloat16)
    low = (table - high.astype(np.float64)).astype(ml_dtypes.bfloat16)
    return high, low


@functools.lru_cache(maxsize=None)
def tables():
    q = np.arange(Q)
    p = np.arange(128)
    eye = np.eye(GROUPS)
    ang_q = 2 * np.pi * np.outer(q, q) / Q
    cos_q, sin_q = np.kron(eye, np.cos(ang_q)), np.kron(eye, np.sin(ang_q))
    first = np.concatenate([cos_q, -sin_q], axis=0)
    last = np.concatenate([cos_q, -sin_q], axis=1)
    ang_t = 2 * np.pi * np.outer(q, p) / NT
    twiddle = np.concatenate([np.tile(np.cos(ang_t), (GROUPS, 1)), np.tile(np.sin(ang_t), (GROUPS, 1))], axis=0)
    ang_p = 2 * np.pi * np.outer(p, np.arange(BINS) - 1) / 128
    cos_p, sin_p = np.cos(ang_p), np.sin(ang_p)
    second = np.block([[cos_p, -sin_p], [sin_p, cos_p]])
    third = np.block([[cos_p.T, sin_p.T], [-sin_p.T, cos_p.T]])
    tri = np.concatenate([
        np.kron(eye, np.ones((Q, Q))),
        np.kron(eye, (q[None, :] >= q[:, None]).astype(float)),
        np.kron(eye, (q[None, :] <= q[:, None]).astype(float)),
    ], axis=0)
    out = []
    for table in (first, second, third, last):
        for piece in split_const(table):
            out.extend(piece[:, at:at + 128] for at in range(0, piece.shape[1], 128))
    out.append(tri.astype(ml_dtypes.bfloat16))
    return [np.concatenate(out, axis=0), twiddle.astype(np.float32)]


def parts2(x):
    high = x.astype(bf16)
    return high, (x - high.astype(f32)).astype(bf16)


def parts3(x):
    high = x.astype(bf16)
    rest = x - high.astype(f32)
    mid = rest.astype(bf16)
    return high, mid, (rest - mid.astype(f32)).astype(bf16)


def dot(a, b):
    return jnp.dot(a, b, preferred_element_type=f32)


def right_product(x, high, low):
    xh, xl = parts2(x)
    return dot(jnp.concatenate([xl, xh, xh], axis=1), jnp.concatenate([high, low, high], axis=0))


def left_product(high, low, x):
    xh, xl = parts2(x)
    return dot(jnp.concatenate([high, low, high], axis=1), jnp.concatenate([xl, xh, xh], axis=0))


def whiten_kernel(alive, starts, halves, x_ref, mats, twid_ref, out_ref, spread_ref, sig, pad):
    lane = lax.broadcasted_iota(jnp.int32, (Q, 128), 1)
    sig[...] = jnp.zeros_like(sig)
    pad[...] = jnp.zeros_like(pad)
    normed = []
    for r in range(2):
        gate = alive[r].astype(f32)
        half = halves[r]
        for s in range(2):
            base = (r * 2 + s) * 48
            for h in range(2):
                piece = x_ref[pl.ds(s * 4 + r * 2 + h, 16, stride=8), :]
                sig[pl.ds(base + h, 16, stride=2), :] = piece * gate
            start = starts[s]
            whole = start // 128
            part = start % 128
            here = sig[pl.ds(base + whole, Q), :]
            after = sig[pl.ds(base + whole + 1, Q), :]
            turn = lax.rem(128 - part, 128)
            moved = jnp.where(lane + part < 128, pltpu.roll(here, turn, 1), pltpu.roll(after, turn, 1))
            pad[pl.ds(base + 8, Q), :] = moved
        row = lax.broadcasted_iota(jnp.int32, (128, 128), 0)
        col = lax.broadcasted_iota(jnp.int32, (128, 128), 1)
        gap = row - col
        bands = (gap >= 128 - half, jnp.abs(gap) <= half, -gap >= 128 - half)
        terms, weights = [], []
        signal = jnp.concatenate([pad[pl.ds((r * 2 + s) * 48 + 8, Q), :] for s in range(2)], axis=0)
        for k, band in enumerate(bands):
            weight = jnp.where(band, 1.0, 0.0).astype(bf16)
            value = jnp.concatenate([pad[pl.ds((r * 2 + s) * 48 + 7 + k, Q), :] for s in range(2)], axis=0)
            terms.extend(parts3(jnp.abs(value)))
            weights.extend([weight] * 3)
        total = dot(jnp.concatenate(terms, axis=1), jnp.concatenate(weights, axis=0))
        level = total / (2 * half + 1).astype(f32)
        normed.append(signal / (level + TINY))
    x = jnp.concatenate(normed, axis=0)
    first_h, first_l, second_h, second_l = (mats[k * 256:(k + 1) * 256, :] for k in range(4))
    third_h, third_l, last_h, last_l = (
        jnp.concatenate([mats[k * 256:k * 256 + 128, :], mats[k * 256 + 128:(k + 1) * 256, :]], axis=1)
        for k in range(4, 8))
    cos_t = twid_ref[0:128, :]
    sin_t = twid_ref[128:256, :]
    stage = left_product(first_h, first_l, x)
    re, im = stage[0:128], stage[128:256]
    turned = jnp.concatenate([re * cos_t + im * sin_t, im * cos_t - re * sin_t], axis=1)
    spec = right_product(turned, second_h, second_l)
    square = spec * spec
    size = jnp.sqrt(square + pltpu.roll(square, BINS, 1))
    tri = mats[2048:2432, :]
    sums = dot(jnp.concatenate([tri] * 3, axis=1), jnp.concatenate(parts3(size), axis=0))
    smooth = (sums[0:128] + pltpu.roll(sums[128:256], 1, 1) + pltpu.roll(sums[256:384], 127, 1)) / 65.0
    k1 = lax.broadcasted_iota(jnp.int32, (128, 128), 0) % Q
    jj = lax.broadcasted_iota(jnp.int32, (128, 128), 1) % BINS
    bins = k1 + Q * (jj - 1)
    band = (bins >= BAND_LO) & (bins <= BAND_HI)
    gain = jnp.where(band, 2.0 / math.sqrt(NT), 0.0) / (smooth + TINY)
    stage = right_product(spec * gain, third_h, third_l)
    re, im = stage[:, 0:128], stage[:, 128:256]
    turned = jnp.concatenate([re * cos_t - im * sin_t, im * cos_t + re * sin_t], axis=0)
    white = left_product(last_h, last_l, turned)
    rolled = pltpu.roll(white, 64, 1)
    for r in range(2):
        sig[pl.ds(r * 40, Q), :] = white[r * 64:r * 64 + Q]
        pad[pl.ds(r * 48 + 8, Q), :] = rolled[r * 64 + Q:r * 64 + 2 * Q]
        pad[pl.ds(r * 48 + 40, 8), :] = jnp.zeros((8, 128), f32)
        pad[pl.ds(r * 48, 8), :] = jnp.zeros((8, 128), f32)
    low = lax.broadcasted_iota(jnp.int32, (2, 128), 1) < 64
    for m in range(2 * Q + 1):
        if m < Q:
            value = sig[pl.ds(m, 2, stride=40), :]
        else:
            value = jnp.where(low, pad[pl.ds(7 + m - Q, 2, stride=48), :], pad[pl.ds(8 + m - Q, 2, stride=48), :])
        value = value.astype(bf16)
        out_ref[:, m * 128:(m + 1) * 128] = value
        for e in range(16):
            spread_ref[e, :, m * 128:(m + 1) * 128] = value


def whiten(x, alive, starts, halves):
    consts = [jnp.asarray(t) for t in tables()]
    smem = pl.BlockSpec(memory_space=pltpu.SMEM)
    vmem = pl.BlockSpec(memory_space=pltpu.VMEM)
    return pl.pallas_call(
        whiten_kernel,
        out_shape=(jax.ShapeDtypeStruct((2, LINE), bf16), jax.ShapeDtypeStruct((16, 2, LINE), bf16)),
        in_specs=[smem] * 3 + [vmem] * 3,
        out_specs=(vmem, vmem),
        scratch_shapes=[pltpu.VMEM((4 * 48, 128), f32), pltpu.VMEM((4 * 48, 128), f32)],
        name="whiten",
    )(alive, starts, halves, x, *consts)


def load_lines(ref, line, first, last, to):
    for k in range(16):
        line[2 * k:2 * k + 2, to:to + last - first] = ref[k, :, first:last]


def corr_kernel(rows_ref, *rest):
    cols, (out_ref, held, sems, xi, xj, acc, left0, right0, left1, right1, tall, form) = rest[:-12], rest[-12:]
    copies, at = [], 0
    for k, ref in enumerate(cols):
        copies.append(pltpu.make_async_copy(ref, held.at[at:at + ref.shape[0]], sems.at[k]))
        copies[-1].start()
        at += ref.shape[0]
    wide = CHUNK + 256
    slots = ((left0, right0), (left1, right1))

    def expand(step):
        left, right = slots[step % 2]
        for ref, line in ((rows_ref, xi), (held, xj)):
            if step == 0:
                if ref is held:
                    for copy in copies:
                        copy.wait()
                load_lines(ref, line, LINE - 128, LINE, 0)
            first = step * CHUNK + 128 if step else 0
            last = min((step + 1) * CHUNK + 128, LINE)
            load_lines(ref, line, first, last, 128 + first)
            if last == LINE:
                line[:, 128 + LINE:256 + LINE] = line[:, 128:256]
        line_i = xi[:, step * CHUNK:step * CHUNK + wide]
        line_j = xj[:, step * CHUNK:step * CHUNK + wide]
        for a in range(A_BLOCKS + 1):
            shift = (STEP * a - LAG) % wide
            moved = pltpu.roll(line_i, shift, 1) if shift else line_i
            left[a * 32:(a + 1) * 32, :] = moved[:, 128:128 + CHUNK]
        for b in range(STEP):
            moved = pltpu.roll(line_j, wide - b, 1) if b else line_j
            right[b * 32:(b + 1) * 32, :] = moved[:, 128:128 + CHUNK]

    expand(0)
    for step in range(LINE // CHUNK):
        if step + 1 < LINE // CHUNK:
            expand(step + 1)
        left, right = slots[step % 2]
        add = lax.dot_general(left[...], right[...], (((1,), (1,)), ((), ())), preferred_element_type=f32)
        acc[...] = add if step == 0 else acc[...] + add

    scale = 1.0 / math.sqrt(2 * NT)
    for bh in range(4):
        tall[bh * 288:(bh + 1) * 288, :] = acc[:, bh * 128:(bh + 1) * 128] * scale
    form[64:72, :] = jnp.zeros((8, 128), f32)
    for t in range(16):
        for bh in range(4):
            for r in range(2):
                form[bh * 16 + r * 8:bh * 16 + r * 8 + 8, :] = tall[pl.ds(bh * 288 + t * 2 + r, 8, stride=32), :]
        form[64:66, :] = tall[256 + t * 2:258 + t * 2, :]
        out_ref[t] = form[...].astype(bf16)


def correlate(rows_in, cols_in):
    vmem = pl.BlockSpec(memory_space=pltpu.VMEM)
    rows = 32 * (A_BLOCKS + 1)
    cols = 32 * STEP
    return pl.pallas_call(
        corr_kernel,
        out_shape=jax.ShapeDtypeStruct((16, 72, 128), bf16),
        in_specs=[vmem] + [pl.BlockSpec(memory_space=pl.ANY)] * len(cols_in),
        out_specs=vmem,
        scratch_shapes=[
            pltpu.VMEM((16, 2, LINE), bf16), pltpu.SemaphoreType.DMA((len(cols_in),)),
            pltpu.VMEM((32, LINE + 256), bf16), pltpu.VMEM((32, LINE + 256), bf16),
            pltpu.VMEM((rows, cols), f32), pltpu.VMEM((rows, CHUNK), bf16), pltpu.VMEM((cols, CHUNK), bf16),
            pltpu.VMEM((rows, CHUNK), bf16), pltpu.VMEM((cols, CHUNK), bf16),
            pltpu.VMEM((4 * rows, 128), f32), pltpu.VMEM((72, 128), f32),
        ],
        compiler_params=pltpu.CompilerParams(vmem_limit_bytes=32 << 20),
        cost_estimate=pl.CostEstimate(flops=2 * rows * cols * LINE, bytes_accessed=4 << 20, transcendentals=0),
        name="correlate",
    )(rows_in, *cols_in)


def place_kernel(own, x_ref, perm_ref, out_ref, rows, res):
    lane = lax.broadcasted_iota(jnp.int32, (16, 128), 1) // 32

    def turn(value, by):
        by = by % 128
        return pltpu.roll(value, by, 1) if by else value

    for hi in range(4):
        for bh in range(5):
            source = [x_ref[hi * 4 + lo, bh * 16:bh * 16 + 16, :].astype(f32) if bh < 4 else
                      jnp.concatenate([x_ref[hi * 4 + lo, 64:72, :].astype(f32)] * 2, axis=0) for lo in range(4)]
            for bl in range(4 if bh < 4 else 1):
                value = turn(source[0], -32 * bl)
                for lo in range(1, 4):
                    value = jnp.where(lane == lo, turn(source[lo], 32 * (lo - bl)), value)
                at = (bh * 4 + bl) * 16
                rows[at:at + 16, hi * 128:(hi + 1) * 128] = value.astype(bf16)
    moved = dot(rows[...], perm_ref[...])
    row = lax.broadcasted_iota(jnp.int32, moved.shape, 0)
    col = lax.broadcasted_iota(jnp.int32, moved.shape, 1)
    which = jnp.where(row < 256, (row // 8) % 2, row % 2)
    moved = jnp.where(col == own[0] + which, 0.0, moved)
    for hi in range(4):
        span = slice(hi * 128, (hi + 1) * 128)
        res[hi * 272:(hi + 1) * 272, :] = moved[:, span]
        for b in range(16):
            for a in range(8):
                out_ref[16 * a + b, :, span] = res[pl.ds(hi * 272 + b * 16 + a, 2, stride=8), :].astype(bf16)
        out_ref[128, :, span] = res[hi * 272 + 256:hi * 272 + 258, :].astype(bf16)


def place(own, x, perm):
    smem = pl.BlockSpec(memory_space=pltpu.SMEM)
    vmem = pl.BlockSpec(memory_space=pltpu.VMEM)
    return pl.pallas_call(
        place_kernel,
        out_shape=jax.ShapeDtypeStruct((129, 2, 512), bf16),
        in_specs=[smem, vmem, vmem],
        out_specs=vmem,
        scratch_shapes=[pltpu.VMEM((272, 512), bf16), pltpu.VMEM((4 * 272, 128), f32)],
        compiler_params=pltpu.CompilerParams(vmem_limit_bytes=16 << 20),
        name="place",
    )(own, x, perm)


PLANE = ("yl", "x", "yh")
SLABS = ("x", "yh", "core")


def crossed(value):
    return lax.ppermute(value, "core", [(0, 1), (1, 0)])


def shed(value, by):
    pairs = []
    for z in range(8):
        pairs.append((z * 2, (z + by) % 8 * 2))
        pairs.append((z * 2 + 1, (z - by) % 8 * 2 + 1))
    return lax.ppermute(value, ("z", "core"), pairs)


def columns_by_hops(white, other):
    own_up, other_up = shed(white, 1), shed(other, 1)
    one = jnp.concatenate([own_up, other_up], axis=0)
    more = shed(jnp.concatenate([white, other, own_up, other_up], axis=0), 2)
    four = shed(more[2:4], 1)
    return white, other, one, more, four, crossed(one), crossed(more)


def on_device(raw, alive, seg_start, norm_half):
    z, yl, x, yh, core = (lax.axis_index(axis) for axis in ("z", "yl", "x", "yh", "core"))
    sent = raw.reshape(2, 16, 2, 2, 128).transpose(1, 0, 2, 3, 4).reshape(16, 8, 128)
    traces = lax.all_to_all(sent, SLABS, split_axis=0, concat_axis=0, tiled=True).reshape(128, 128)
    white, spread = whiten(traces, alive, seg_start, norm_half)
    rows = lax.all_to_all(spread, PLANE, split_axis=0, concat_axis=0, tiled=True)
    white = white[None]
    other = crossed(white)
    block = correlate(rows, columns_by_hops(white, other))
    back = lax.all_to_all(block, PLANE, split_axis=0, concat_axis=0, tiled=True)
    k = np.arange(512)
    e, pair_id, side = k // 32, (k // 4) % 8, (k // 2) % 2
    step = np.array([0, 1, 2, 3, 4, -1, -2, -3])[pair_id]
    side = side ^ (pair_id >= 5)
    fixed = (e // 8) * 32 + ((e // 2) % 4) * 8 + (e % 2) * 4 + k % 2
    from_z = (z + jnp.asarray(step, jnp.int32) * (2 * core - 1)) & 7
    target = from_z * 64 + jnp.asarray(fixed, jnp.int32) + (core ^ jnp.asarray(side, jnp.int32)) * 2
    k = lax.iota(jnp.int32, 512)
    perm = (target[:, None] == k[None, :]).astype(bf16)
    own = (((z * 2 + yl) * 16 + x * 4 + yh * 2 + core) * 2).astype(jnp.int32).reshape(1)
    return place(own, back, perm).transpose(1, 0, 2)


def solution(mesh):
    fine = Mesh(mesh.devices.reshape(8, 2, 4, 2, 2), ("z", "yl", "x", "yh", "core"))
    both = ("z", "yl", "x", "yh", "core")
    return jax.shard_map(
        on_device,
        mesh=fine,
        in_specs=(P(None, ("z", "yl"), SLABS), P(both), P(), P(both)),
        out_specs=P(both, None, None),
        check_vma=False,
    )
```

```python
import functools
import math

import jax
import jax.numpy as jnp
import ml_dtypes
import numpy as np
from jax import lax
from jax.experimental import pallas as pl
from jax.experimental.pallas import tpu as pltpu
from jax.sharding import Mesh, PartitionSpec as P

LAG = 64
TINY = 1e-05
NT = 4096
Q = 32
GROUPS = 4
LINE = 2 * (NT + LAG)
STEP = 16
A_BLOCKS = 2 * LAG // STEP
CHUNK = 13 * 128
BAND_LO = 16
BAND_HI = 1638
BINS = 64

bf16 = jnp.bfloat16
f32 = jnp.float32


def split_const(table):
    high = table.astype(ml_dtypes.bfloat16)
    low = (table - high.astype(np.float64)).astype(ml_dtypes.bfloat16)
    return high, low


@functools.lru_cache(maxsize=None)
def tables():
    q = np.arange(Q)
    p = np.arange(128)
    eye = np.eye(GROUPS)
    ang_q = 2 * np.pi * np.outer(q, q) / Q
    cos_q, sin_q = np.kron(eye, np.cos(ang_q)), np.kron(eye, np.sin(ang_q))
    first = np.concatenate([cos_q, -sin_q], axis=0)
    last = np.concatenate([cos_q, -sin_q], axis=1)
    ang_t = 2 * np.pi * np.outer(q, p) / NT
    twiddle = np.concatenate([np.tile(np.cos(ang_t), (GROUPS, 1)), np.tile(np.sin(ang_t), (GROUPS, 1))], axis=0)
    ang_p = 2 * np.pi * np.outer(p, np.arange(BINS) - 1) / 128
    cos_p, sin_p = np.cos(ang_p), np.sin(ang_p)
    second = np.block([[cos_p, -sin_p], [sin_p, cos_p]])
    third = np.block([[cos_p.T, sin_p.T], [-sin_p.T, cos_p.T]])
    tri = np.concatenate([
        np.kron(eye, np.ones((Q, Q))),
        np.kron(eye, (q[None, :] >= q[:, None]).astype(float)),
        np.kron(eye, (q[None, :] <= q[:, None]).astype(float)),
    ], axis=0)
    out = []
    for table in (first, second, third, last):
        for piece in split_const(table):
            out.extend(piece[:, at:at + 128] for at in range(0, piece.shape[1], 128))
    out.append(tri.astype(ml_dtypes.bfloat16))
    return [np.concatenate(out, axis=0), twiddle.astype(np.float32)]


def parts2(x):
    high = x.astype(bf16)
    return high, (x - high.astype(f32)).astype(bf16)


def parts3(x):
    high = x.astype(bf16)
    rest = x - high.astype(f32)
    mid = rest.astype(bf16)
    return high, mid, (rest - mid.astype(f32)).astype(bf16)


def dot(a, b):
    return jnp.dot(a, b, preferred_element_type=f32)


def right_product(x, high, low):
    xh, xl = parts2(x)
    return dot(jnp.concatenate([xl, xh, xh], axis=1), jnp.concatenate([high, low, high], axis=0))


def left_product(high, low, x):
    xh, xl = parts2(x)
    return dot(jnp.concatenate([high, low, high], axis=1), jnp.concatenate([xl, xh, xh], axis=0))


def whiten_kernel(alive, starts, halves, x_ref, mats, twid_ref, out_ref, spread_ref, sig, pad):
    lane = lax.broadcasted_iota(jnp.int32, (Q, 128), 1)
    sig[...] = jnp.zeros_like(sig)
    pad[...] = jnp.zeros_like(pad)
    normed = []
    for r in range(2):
        gate = alive[r].astype(f32)
        half = halves[r]
        for s in range(2):
            base = (r * 2 + s) * 48
            for h in range(2):
                piece = x_ref[pl.ds(s * 4 + r * 2 + h, 16, stride=8), :]
                sig[pl.ds(base + h, 16, stride=2), :] = piece * gate
            start = starts[s]
            whole = start // 128
            part = start % 128
            here = sig[pl.ds(base + whole, Q), :]
            after = sig[pl.ds(base + whole + 1, Q), :]
            turn = lax.rem(128 - part, 128)
            moved = jnp.where(lane + part < 128, pltpu.roll(here, turn, 1), pltpu.roll(after, turn, 1))
            pad[pl.ds(base + 8, Q), :] = moved
        row = lax.broadcasted_iota(jnp.int32, (128, 128), 0)
        col = lax.broadcasted_iota(jnp.int32, (128, 128), 1)
        gap = row - col
        bands = (gap >= 128 - half, jnp.abs(gap) <= half, -gap >= 128 - half)
        terms, weights = [], []
        signal = jnp.concatenate([pad[pl.ds((r * 2 + s) * 48 + 8, Q), :] for s in range(2)], axis=0)
        for k, band in enumerate(bands):
            weight = jnp.where(band, 1.0, 0.0).astype(bf16)
            value = jnp.concatenate([pad[pl.ds((r * 2 + s) * 48 + 7 + k, Q), :] for s in range(2)], axis=0)
            terms.extend(parts3(jnp.abs(value)))
            weights.extend([weight] * 3)
        total = dot(jnp.concatenate(terms, axis=1), jnp.concatenate(weights, axis=0))
        level = total / (2 * half + 1).astype(f32)
        normed.append(signal / (level + TINY))
    x = jnp.concatenate(normed, axis=0)
    first_h, first_l, second_h, second_l = (mats[k * 256:(k + 1) * 256, :] for k in range(4))
    third_h, third_l, last_h, last_l = (
        jnp.concatenate([mats[k * 256:k * 256 + 128, :], mats[k * 256 + 128:(k + 1) * 256, :]], axis=1)
        for k in range(4, 8))
    cos_t = twid_ref[0:128, :]
    sin_t = twid_ref[128:256, :]
    stage = left_product(first_h, first_l, x)
    re, im = stage[0:128], stage[128:256]
    turned = jnp.concatenate([re * cos_t + im * sin_t, im * cos_t - re * sin_t], axis=1)
    spec = right_product(turned, second_h, second_l)
    square = spec * spec
    size = jnp.sqrt(square + pltpu.roll(square, BINS, 1))
    tri = mats[2048:2432, :]
    sums = dot(jnp.concatenate([tri] * 3, axis=1), jnp.concatenate(parts3(size), axis=0))
    smooth = (sums[0:128] + pltpu.roll(sums[128:256], 1, 1) + pltpu.roll(sums[256:384], 127, 1)) / 65.0
    k1 = lax.broadcasted_iota(jnp.int32, (128, 128), 0) % Q
    jj = lax.broadcasted_iota(jnp.int32, (128, 128), 1) % BINS
    bins = k1 + Q * (jj - 1)
    band = (bins >= BAND_LO) & (bins <= BAND_HI)
    gain = jnp.where(band, 2.0 / math.sqrt(NT), 0.0) / (smooth + TINY)
    stage = right_product(spec * gain, third_h, third_l)
    re, im = stage[:, 0:128], stage[:, 128:256]
    turned = jnp.concatenate([re * cos_t - im * sin_t, im * cos_t + re * sin_t], axis=0)
    white = left_product(last_h, last_l, turned)
    rolled = pltpu.roll(white, 64, 1)
    for r in range(2):
        sig[pl.ds(r * 40, Q), :] = white[r * 64:r * 64 + Q]
        pad[pl.ds(r * 48 + 8, Q), :] = rolled[r * 64 + Q:r * 64 + 2 * Q]
        pad[pl.ds(r * 48 + 40, 8), :] = jnp.zeros((8, 128), f32)
        pad[pl.ds(r * 48, 8), :] = jnp.zeros((8, 128), f32)
    low = lax.broadcasted_iota(jnp.int32, (2, 128), 1) < 64
    for m in range(2 * Q + 1):
        if m < Q:
            value = sig[pl.ds(m, 2, stride=40), :]
        else:
            value = jnp.where(low, pad[pl.ds(7 + m - Q, 2, stride=48), :], pad[pl.ds(8 + m - Q, 2, stride=48), :])
        value = value.astype(bf16)
        out_ref[:, m * 128:(m + 1) * 128] = value
        for e in range(16):
            spread_ref[e, :, m * 128:(m + 1) * 128] = value


def whiten(x, alive, starts, halves):
    consts = [jnp.asarray(t) for t in tables()]
    smem = pl.BlockSpec(memory_space=pltpu.SMEM)
    vmem = pl.BlockSpec(memory_space=pltpu.VMEM)
    return pl.pallas_call(
        whiten_kernel,
        out_shape=(jax.ShapeDtypeStruct((2, LINE), bf16), jax.ShapeDtypeStruct((16, 2, LINE), bf16)),
        in_specs=[smem] * 3 + [vmem] * 3,
        out_specs=(vmem, vmem),
        scratch_shapes=[pltpu.VMEM((4 * 48, 128), f32), pltpu.VMEM((4 * 48, 128), f32)],
        name="whiten",
    )(alive, starts, halves, x, *consts)


def load_lines(ref, line, first, last, to):
    if len(ref.shape) == 2:
        line[:, to:to + last - first] = ref[:, first:last]
        return
    for k in range(16):
        line[2 * k:2 * k + 2, to:to + last - first] = ref[k, :, first:last]


def corr_kernel(rows_ref, *rest):
    cols, (out_ref, held, sems, xi, xj, acc, left0, right0, left1, right1, tall, form) = rest[:-12], rest[-12:]
    copies, at = [], 0
    for k, ref in enumerate(cols):
        copies.append(pltpu.make_async_copy(ref, held.at[at:at + ref.shape[0]], sems.at[k]))
        copies[-1].start()
        at += ref.shape[0]
    wide = CHUNK + 256
    slots = ((left0, right0), (left1, right1))

    def expand(step):
        left, right = slots[step % 2]
        for ref, line in ((rows_ref, xi), (held, xj)):
            if step == 0:
                if ref is held:
                    for copy in copies:
                        copy.wait()
                load_lines(ref, line, LINE - 128, LINE, 0)
            first = step * CHUNK + 128 if step else 0
            last = min((step + 1) * CHUNK + 128, LINE)
            load_lines(ref, line, first, last, 128 + first)
            if last == LINE:
                line[:, 128 + LINE:256 + LINE] = line[:, 128:256]
        line_i = xi[:, step * CHUNK:step * CHUNK + wide]
        line_j = xj[:, step * CHUNK:step * CHUNK + wide]
        for a in range(A_BLOCKS + 1):
            shift = (STEP * a - LAG) % wide
            moved = pltpu.roll(line_i, shift, 1) if shift else line_i
            left[a * 32:(a + 1) * 32, :] = moved[:, 128:128 + CHUNK]
        for b in range(STEP):
            moved = pltpu.roll(line_j, wide - b, 1) if b else line_j
            right[b * 32:(b + 1) * 32, :] = moved[:, 128:128 + CHUNK]

    expand(0)
    for step in range(LINE // CHUNK):
        if step + 1 < LINE // CHUNK:
            expand(step + 1)
        left, right = slots[step % 2]
        add = lax.dot_general(left[...], right[...], (((1,), (1,)), ((), ())), preferred_element_type=f32)
        acc[...] = add if step == 0 else acc[...] + add

    scale = 1.0 / math.sqrt(2 * NT)
    for bh in range(4):
        tall[bh * 288:(bh + 1) * 288, :] = acc[:, bh * 128:(bh + 1) * 128] * scale
    form[64:72, :] = jnp.zeros((8, 128), f32)
    for t in range(16):
        for bh in range(4):
            for r in range(2):
                form[bh * 16 + r * 8:bh * 16 + r * 8 + 8, :] = tall[pl.ds(bh * 288 + t * 2 + r, 8, stride=32), :]
        form[64:66, :] = tall[256 + t * 2:258 + t * 2, :]
        out_ref[t] = form[...].astype(bf16)


def correlate(rows_in, cols_in):
    vmem = pl.BlockSpec(memory_space=pltpu.VMEM)
    rows = 32 * (A_BLOCKS + 1)
    cols = 32 * STEP
    return pl.pallas_call(
        corr_kernel,
        out_shape=jax.ShapeDtypeStruct((16, 72, 128), bf16),
        in_specs=[vmem] + [pl.BlockSpec(memory_space=pl.ANY)] * len(cols_in),
        out_specs=vmem,
        scratch_shapes=[
            pltpu.VMEM((16, 2, LINE), bf16), pltpu.SemaphoreType.DMA((len(cols_in),)),
            pltpu.VMEM((32, LINE + 256), bf16), pltpu.VMEM((32, LINE + 256), bf16),
            pltpu.VMEM((rows, cols), f32), pltpu.VMEM((rows, CHUNK), bf16), pltpu.VMEM((cols, CHUNK), bf16),
            pltpu.VMEM((rows, CHUNK), bf16), pltpu.VMEM((cols, CHUNK), bf16),
            pltpu.VMEM((4 * rows, 128), f32), pltpu.VMEM((72, 128), f32),
        ],
        compiler_params=pltpu.CompilerParams(vmem_limit_bytes=32 << 20),
        cost_estimate=pl.CostEstimate(flops=2 * rows * cols * LINE, bytes_accessed=4 << 20, transcendentals=0),
        name="correlate",
    )(rows_in.reshape(32, LINE), *cols_in)


def place_kernel(own, x_ref, perm_ref, out_ref, rows, res):
    lane = lax.broadcasted_iota(jnp.int32, (16, 128), 1) // 32

    def turn(value, by):
        by = by % 128
        return pltpu.roll(value, by, 1) if by else value

    for hi in range(4):
        for bh in range(5):
            source = [x_ref[hi * 4 + lo, bh * 16:bh * 16 + 16, :].astype(f32) if bh < 4 else
                      jnp.concatenate([x_ref[hi * 4 + lo, 64:72, :].astype(f32)] * 2, axis=0) for lo in range(4)]
            for bl in range(4 if bh < 4 else 1):
                value = turn(source[0], -32 * bl)
                for lo in range(1, 4):
                    value = jnp.where(lane == lo, turn(source[lo], 32 * (lo - bl)), value)
                at = (bh * 4 + bl) * 16
                rows[at:at + 16, hi * 128:(hi + 1) * 128] = value.astype(bf16)
    moved = dot(rows[...], perm_ref[...])
    row = lax.broadcasted_iota(jnp.int32, moved.shape, 0)
    col = lax.broadcasted_iota(jnp.int32, moved.shape, 1)
    which = jnp.where(row < 256, (row // 8) % 2, row % 2)
    moved = jnp.where(col == own[0] + which, 0.0, moved)
    for hi in range(4):
        span = slice(hi * 128, (hi + 1) * 128)
        res[hi * 272:(hi + 1) * 272, :] = moved[:, span]
        for b in range(16):
            for a in range(8):
                out_ref[16 * a + b, :, span] = res[pl.ds(hi * 272 + b * 16 + a, 2, stride=8), :].astype(bf16)
        out_ref[128, :, span] = res[hi * 272 + 256:hi * 272 + 258, :].astype(bf16)


def place(own, x, perm):
    smem = pl.BlockSpec(memory_space=pltpu.SMEM)
    vmem = pl.BlockSpec(memory_space=pltpu.VMEM)
    return pl.pallas_call(
        place_kernel,
        out_shape=jax.ShapeDtypeStruct((129, 2, 512), bf16),
        in_specs=[smem, vmem, vmem],
        out_specs=vmem,
        scratch_shapes=[pltpu.VMEM((272, 512), bf16), pltpu.VMEM((4 * 272, 128), f32)],
        compiler_params=pltpu.CompilerParams(vmem_limit_bytes=16 << 20),
        name="place",
    )(own, x, perm)


PLANE = ("yl", "x", "yh")
SLABS = ("x", "yh", "core")


def crossed(value):
    return lax.ppermute(value, "core", [(0, 1), (1, 0)])


def shed(value, by):
    pairs = []
    for z in range(8):
        pairs.append((z * 2, (z + by) % 8 * 2))
        pairs.append((z * 2 + 1, (z - by) % 8 * 2 + 1))
    return lax.ppermute(value, ("z", "core"), pairs)


def columns_by_hops(white, other):
    own_up, other_up = shed(white, 1), shed(other, 1)
    one = jnp.concatenate([own_up, other_up], axis=0)
    more = shed(jnp.concatenate([white, other, own_up, other_up], axis=0), 2)
    four = shed(more[2:4], 1)
    return white, other, one, more, four, crossed(one), crossed(more)


def on_device(raw, alive, seg_start, norm_half):
    z, yl, x, yh, core = (lax.axis_index(axis) for axis in ("z", "yl", "x", "yh", "core"))
    sent = raw.reshape(2, 16, 2, 2, 128).transpose(1, 0, 2, 3, 4).reshape(16, 8, 128)
    traces = lax.all_to_all(sent, SLABS, split_axis=0, concat_axis=0, tiled=True).reshape(128, 128)
    white, spread = whiten(traces, alive, seg_start, norm_half)
    rows = lax.all_to_all(spread, PLANE, split_axis=0, concat_axis=0, tiled=True)
    white = white[None]
    other = crossed(white)
    block = correlate(rows, columns_by_hops(white, other))
    back = lax.all_to_all(block, PLANE, split_axis=0, concat_axis=0, tiled=True)
    k = np.arange(512)
    e, pair_id, side = k // 32, (k // 4) % 8, (k // 2) % 2
    step = np.array([0, 1, 2, 3, 4, -1, -2, -3])[pair_id]
    side = side ^ (pair_id >= 5)
    fixed = (e // 8) * 32 + ((e // 2) % 4) * 8 + (e % 2) * 4 + k % 2
    from_z = (z + jnp.asarray(step, jnp.int32) * (2 * core - 1)) & 7
    target = from_z * 64 + jnp.asarray(fixed, jnp.int32) + (core ^ jnp.asarray(side, jnp.int32)) * 2
    k = lax.iota(jnp.int32, 512)
    perm = (target[:, None] == k[None, :]).astype(bf16)
    own = (((z * 2 + yl) * 16 + x * 4 + yh * 2 + core) * 2).astype(jnp.int32).reshape(1)
    return place(own, back, perm).transpose(1, 0, 2)


def solution(mesh):
    fine = Mesh(mesh.devices.reshape(8, 2, 4, 2, 2), ("z", "yl", "x", "yh", "core"))
    both = ("z", "yl", "x", "yh", "core")
    return jax.shard_map(
        on_device,
        mesh=fine,
        in_specs=(P(None, ("z", "yl"), SLABS), P(both), P(), P(both)),
        out_specs=P(both, None, None),
        check_vma=False,
    )
```
